32 devices in a mesh: seq: 4 (over x, core), batch: 8 (over z, y).
Axes of the slice: x: 2, y: 2, z: 4, core: 2. Of those that a mesh axis runs over, the one named last changes fastest.
Arguments:
- tokens: bfloat16 [8, 1024, 1024], P('batch', 'seq'), may hold values from -6 to 6
- w_query: bfloat16 [1024, 1024], P(('seq', 'batch')), may hold values from -0.25 to 0.25
- w_key: bfloat16 [1024, 1024], P(('seq', 'batch')), may hold values from -0.25 to 0.25
- w_value: bfloat16 [1024, 1024], P(('seq', 'batch')), may hold values from -0.1875 to 0.1875
- w_out: bfloat16 [1024, 1024], P(('seq', 'batch')), may hold values from -0.375 to 0.375
- gain_attn: bfloat16 [1024], P(('seq', 'batch')), may hold values from 0.25 to 1.75
- w_gate: bfloat16 [1024, 4096], P(('seq', 'batch')), may hold values from -0.1875 to 0.1875
- w_up: bfloat16 [1024, 4096], P(('seq', 'batch')), may hold values from -0.1875 to 0.1875
- w_down: bfloat16 [4096, 1024], P(('seq', 'batch')), may hold values from -0.125 to 0.125
- gain_ffn: bfloat16 [1024], P(('seq', 'batch')), may hold values from 0.25 to 1.75
- counts: int32 [8, 4], P('batch'), may hold values from 0 to 256, as said below
- cotangent: bfloat16 [8, 1024, 1024], P('batch', 'seq'), may hold values from -6 to 6
Outputs:
- block_output: bfloat16 [8, 1024, 1024], P('batch', 'seq')
- input_grad: float32 [8, 1024, 1024], P('batch', 'seq')
- grad_w_query: float32 [1024, 1024], P(('seq', 'batch'))
- grad_w_key: float32 [1024, 1024], P(('seq', 'batch'))
- grad_w_value: float32 [1024, 1024], P(('seq', 'batch'))
- grad_w_out: float32 [1024, 1024], P(('seq', 'batch'))
- grad_gain_attn: float32 [1024], P(('seq', 'batch'))
- grad_w_gate: float32 [1024, 4096], P(('seq', 'batch'))
- grad_w_up: float32 [1024, 4096], P(('seq', 'batch'))
- grad_w_down: float32 [4096, 1024], P(('seq', 'batch'))
- grad_gain_ffn: float32 [1024], P(('seq', 'batch'))
The draws below stay inside these ranges and needn't reach their ends.
Inputs may be any that keep to these rules, and one draw needn't show every extreme that they name: counts[s, i] = min(max(L_s - i * 256, 0), 256) for a length L_s of sequence s between 256 and 1024; some sequence has length 1024 and another length 256.
All inputs are finite; a program needn't handle non-finite values.
Results may differ from the reference program's by a relative error of at most 0.017.
Values may be sent and summed in bfloat16 or wider, within the bound.
No kernel may reach another device: no remote copies, remote signals or barrier semaphores. Data moves between devices by JAX's collectives and lax.ppermute only.
A program may use at most 192 MiB of HBM per device.

```python
import math
import jax
import jax.numpy as jnp
from jax import lax

D = 1024
HEADS = 16
HEAD_DIM = 64
FF = 4096
TOK_DEV = 256
SEQ_LEN = 1024
SEQS = 8
N_SEQ = 4


def draw_counts(key, part):
    key_length, key_pick = jax.random.split(key)
    lengths = jax.random.randint(key_length, (SEQS,), TOK_DEV, SEQ_LEN + 1, dtype=jnp.int32)
    chosen = jax.random.permutation(key_pick, SEQS)
    lengths = lengths.at[chosen[0]].set(SEQ_LEN).at[chosen[1]].set(TOK_DEV)
    offsets = jnp.arange(N_SEQ, dtype=jnp.int32) * TOK_DEV
    return jnp.clip(lengths[:, None] - offsets[None, :], 0, TOK_DEV).astype(jnp.int32)


def steps_of(key, dims, pieces, low, largest):
    level, own = 1.0, jax.random.fold_in(key, 6)
    for dim, parts in pieces:
        heights = jnp.exp(jax.random.uniform(jax.random.fold_in(own, dim), (parts,), jnp.float32, low / len(pieces), largest / len(pieces)))
        level = level * jnp.repeat(heights, dims[dim] // parts).reshape([-1 if axis == dim else 1 for axis in range(len(dims))])
    return level


def scatter_about(key, dims, spread, most, cuts=(), kind=jnp.bfloat16):
    loudness = steps_of(key, dims, cuts, -0.22, 0.18) if cuts else 1.0
    array = jax.random.normal(key, dims, jnp.float32) * spread * loudness
    return jnp.minimum(jnp.maximum(array, -most), most).astype(kind)


def setup_inputs(seed: int = 0) -> dict:
    streams_of = jax.random.split(jax.random.key(seed), 13)
    tokens = scatter_about(streams_of[0], (SEQS, SEQ_LEN, D), 1.0, 6.0, ((0, 8), (1, 4)))
    w_query = scatter_about(streams_of[1], (D, D), (D // 2) ** -0.5, 0.25, ((0, 32),))
    w_key = scatter_about(streams_of[2], (D, D), (D // 2) ** -0.5, 0.25, ((0, 32),))
    w_value = scatter_about(streams_of[3], (D, D), D ** -0.5, 0.1875, ((0, 32),))
    w_out = scatter_about(streams_of[4], (D, D), (D // 4) ** -0.5, 0.375, ((0, 32),))
    gain_attn = jnp.clip(1.0 + 0.15 * jax.random.normal(streams_of[5], (D,), jnp.float32), 0.25, 1.75).astype(jnp.bfloat16)
    w_gate = scatter_about(streams_of[6], (D, FF), D ** -0.5, 0.1875, ((0, 32),))
    w_up = scatter_about(streams_of[7], (D, FF), D ** -0.5, 0.1875, ((0, 32),))
    w_down = scatter_about(streams_of[8], (FF, D), (FF // 2) ** -0.5, 0.125, ((0, 32),))
    gain_ffn = jnp.clip(1.0 + 0.15 * jax.random.normal(streams_of[9], (D,), jnp.float32), 0.25, 1.75).astype(jnp.bfloat16)
    counts = draw_counts(jax.random.fold_in(streams_of[12], 71), 0)
    cotangent = scatter_about(streams_of[11], (SEQS, SEQ_LEN, D), 1.0, 6.0, ((0, 8), (1, 4)))
    return dict(tokens=tokens, w_query=w_query, w_key=w_key, w_value=w_value, w_out=w_out, gain_attn=gain_attn, w_gate=w_gate, w_up=w_up, w_down=w_down, gain_ffn=gain_ffn, counts=counts, cotangent=cotangent)


@jax.custom_vjp
def low(v):
    return lax.optimization_barrier(v.astype(jnp.bfloat16)).astype(jnp.float32)

@jax.custom_vjp
def low_back(v):
    return v

def low_keep(v):
    return (low(v), None)

def low_pass(kept, grad):
    return (grad,)

def back_keep(v):
    return (v, None)

def back_low(kept, grad):
    return (low(grad),)
low.defvjp(low_keep, low_pass)
low_back.defvjp(back_keep, back_low)
EPSILON = 1e-05

def rms_norm(values, gain):
    return values * lax.rsqrt(lax.optimization_barrier(jnp.mean(values * values, axis=-1, keepdims=True)) + EPSILON) * gain

def matmul(left, right):
    return jnp.dot(left, right, precision=lax.Precision.HIGHEST)

def block_layer(inputs_seq, params, usable):
    w_query, w_key, w_value, w_out, gain_attn, w_gate, w_up, w_down, gain_ffn = params
    score_scale = HEAD_DIM ** (-0.5)
    score_offset = -math.log(SEQ_LEN)
    normed_attn = low(rms_norm(inputs_seq, gain_attn))
    query = low(low_back(matmul(normed_attn, w_query))).reshape(SEQ_LEN, HEADS, HEAD_DIM)
    key = low(low_back(matmul(normed_attn, w_key))).reshape(SEQ_LEN, HEADS, HEAD_DIM)
    value = low(low_back(matmul(normed_attn, w_value))).reshape(SEQ_LEN, HEADS, HEAD_DIM)
    positions = jnp.arange(SEQ_LEN, dtype=jnp.int32)

    def query_block(block_index):
        first_row = (block_index * TOK_DEV).astype(jnp.int32)
        query_rows = lax.dynamic_slice_in_dim(query, first_row, TOK_DEV, 0)
        query_pos = first_row + jnp.arange(TOK_DEV, dtype=jnp.int32)
        scores = jnp.einsum('qhe,khe->hqk', query_rows, key, precision=lax.Precision.HIGHEST) * score_scale + score_offset
        scores = low_back(scores)
        allowed = (positions[None, :] <= query_pos[:, None]) & usable[None, :]
        probs = low(jnp.where(allowed[None], jax.nn.sigmoid(scores), 0.0))
        return jnp.einsum('hqk,khe->qhe', probs, value, precision=lax.Precision.HIGHEST)
    attended = lax.map(jax.checkpoint(query_block), jnp.arange(N_SEQ, dtype=jnp.int32))
    attended = low(low_back(attended.reshape(SEQ_LEN, HEADS * HEAD_DIM)))
    resid = inputs_seq + low_back(matmul(attended, w_out))
    normed_ffn = low(rms_norm(resid, gain_ffn))
    gate = low_back(matmul(normed_ffn, w_gate))
    up_proj = low_back(matmul(normed_ffn, w_up))
    hidden = low(jax.nn.silu(gate) * up_proj)
    return resid + matmul(hidden, w_down)

def reference(tokens, w_query, w_key, w_value, w_out, gain_attn, w_gate, w_up, w_down, gain_ffn, counts, cotangent):
    params = tuple((weight.astype(jnp.float32) for weight in (w_query, w_key, w_value, w_out, gain_attn, w_gate, w_up, w_down, gain_ffn)))
    positions = jnp.arange(SEQ_LEN, dtype=jnp.int32)

    def per_sequence(totals, inputs):
        inputs_seq, cot_seq, count_row = inputs
        usable = positions % TOK_DEV < jnp.repeat(count_row, TOK_DEV, total_repeat_length=SEQ_LEN)
        result, pullback = jax.vjp(lambda given, weights: block_layer(given, weights, usable), inputs_seq.astype(jnp.float32), params)
        grad_input, grad_params = pullback(cot_seq.astype(jnp.float32))
        totals = jax.tree.map(lambda first, second: first + second, totals, grad_params)
        return (totals, (result.astype(jnp.bfloat16), grad_input))
    initial = jax.tree.map(jnp.zeros_like, params)
    finals, (outputs, input_grads) = lax.scan(per_sequence, initial, (tokens, cotangent, counts))
    return (outputs, input_grads, finals[0], finals[1], finals[2], finals[3], finals[4], finals[5], finals[6], finals[7], finals[8])
```

```python
import math

import jax
import jax.numpy as jnp
from jax import lax
from jax.experimental import pallas as pl
from jax.experimental.pallas import tpu as pltpu
from jax.sharding import Mesh
from jax.sharding import PartitionSpec as P

HEADS = 16
EPSILON = 1e-05
TILE = 256
PLANE = ("x", "c", "y")
F32 = jnp.float32
BF16 = jnp.bfloat16


def rms_scale(source):
    return lax.rsqrt(jnp.mean(source * source, axis=-1, keepdims=True) + EPSILON)


def norm_back(incoming, source, gain_full):
    inverse = rms_scale(source)
    scaled = incoming * gain_full
    grad_source = inverse * (
        scaled - source * (inverse * inverse) * jnp.mean(scaled * source, axis=-1, keepdims=True)
    )
    grad_gain = jnp.sum(incoming * source * inverse, axis=0)
    return (grad_source, grad_gain)


def dot(left, right):
    return jnp.dot(left, right, preferred_element_type=F32)


def dot_nt(left, right):
    return lax.dot_general(left, right, (((1,), (1,)), ((), ())), preferred_element_type=F32)


def dot_tn(left, right):
    return lax.dot_general(left, right, (((0,), (0,)), ((), ())), preferred_element_type=F32)


def lane_masks(width, count):
    lane = lax.broadcasted_iota(jnp.int32, (1, width), 1)
    return [(lane // (width // count)) == h for h in range(count)]


def spread(block, masks):
    zero = jnp.zeros_like(block)
    return jnp.concatenate([jnp.where(m, block, zero) for m in masks], axis=0)


def gather_heads(stacked, masks):
    rows = stacked.shape[0] // len(masks)
    total = jnp.where(masks[0], stacked[:rows], 0.0)
    for h in range(1, len(masks)):
        total = jnp.where(masks[h], stacked[h * rows : (h + 1) * rows], total)
    return total


def attn_fwd_kernel(offset, heads, lens_ref, qkv_ref, out_ref):
    length = lens_ref[pl.program_id(0)]
    seq, width = qkv_ref.shape[0], qkv_ref.shape[1] // 3
    scale = (width // heads) ** -0.5
    masks = lane_masks(width, heads)
    for i in range(seq // TILE):
        q = spread(qkv_ref[i * TILE : (i + 1) * TILE, :width] * jnp.asarray(scale, BF16), masks)
        acc = jnp.zeros((heads * TILE, width), F32)
        for j in range(i + 1):
            k = qkv_ref[j * TILE : (j + 1) * TILE, width : 2 * width]
            v = qkv_ref[j * TILE : (j + 1) * TILE, 2 * width :]
            scores = dot_nt(q, k)
            gates = 1.0 / (1.0 + jnp.exp(offset - scores))
            key = lax.broadcasted_iota(jnp.int32, (heads * TILE, TILE), 1)
            allowed = key < length - j * TILE
            if j == i:
                row = lax.broadcasted_iota(jnp.int32, (heads * TILE, TILE), 0) % TILE
                allowed = allowed & (key <= row)
            probs = jnp.where(allowed, gates, 0.0).astype(BF16)
            acc = acc + dot(probs, v)
        out_ref[i * TILE : (i + 1) * TILE, :] = gather_heads(acc, masks).astype(BF16)


def attn_bwd_kernel(offset, heads, lens_ref, qkv_ref, grad_ref, out_ref, dk_ref, dv_ref):
    length = lens_ref[pl.program_id(0)]
    seq, width = qkv_ref.shape[0], qkv_ref.shape[1] // 3
    scale = (width // heads) ** -0.5
    masks = lane_masks(width, heads)
    steps = seq // TILE
    for i in range(steps):
        rows = slice(i * TILE, (i + 1) * TILE)
        q = spread(qkv_ref[rows, :width] * jnp.asarray(scale, BF16), masks)
        grad = spread(grad_ref[rows, :], masks)
        dq = jnp.zeros((heads * TILE, width), F32)
        for j in range(i + 1):
            cols = slice(j * TILE, (j + 1) * TILE)
            k = qkv_ref[cols, width : 2 * width]
            v = qkv_ref[cols, 2 * width :]
            scores = dot_nt(k, q)
            gates = 1.0 / (1.0 + jnp.exp(offset - scores))
            key = lax.broadcasted_iota(jnp.int32, (TILE, heads * TILE), 0)
            allowed = key < length - j * TILE
            if j == i:
                row = lax.broadcasted_iota(jnp.int32, (TILE, heads * TILE), 1) % TILE
                allowed = allowed & (key <= row)
            gates = jnp.where(allowed, gates, 0.0)
            grad_scores = (dot_nt(v, grad) * gates * (1.0 - gates)).astype(BF16)
            dv = dot(gates.astype(BF16), grad)
            dk = dot(grad_scores, q)
            dq = dq + dot_tn(grad_scores, k)
            if i == j:
                dv_ref[cols, :] = dv
                dk_ref[cols, :] = dk
            else:
                dv_ref[cols, :] += dv
                dk_ref[cols, :] += dk
        out_ref[rows, :width] = (gather_heads(dq, masks) * scale).astype(BF16)
    out_ref[:, width : 2 * width] = dk_ref[...].astype(BF16)
    out_ref[:, 2 * width :] = dv_ref[...].astype(BF16)


def attn_fwd(lens, qkv, heads):
    count, seq, wide = qkv.shape
    width = wide // 3
    return pl.pallas_call(
        lambda *refs: attn_fwd_kernel(math.log(seq), heads, *refs),
        out_shape=jax.ShapeDtypeStruct((count, seq, width), BF16),
        grid_spec=pltpu.PrefetchScalarGridSpec(
            num_scalar_prefetch=1,
            grid=(count,),
            in_specs=[pl.BlockSpec((None, seq, wide), lambda b, lens: (b, 0, 0))],
            out_specs=pl.BlockSpec((None, seq, width), lambda b, lens: (b, 0, 0)),
        ),
        cost_estimate=pl.CostEstimate(
            flops=8 * count * seq * seq * width, bytes_accessed=8 * count * seq * width, transcendentals=count * seq * seq * heads
        ),
        name="attn_fwd",
    )(lens, qkv)


def attn_bwd(lens, qkv, grad, heads):
    count, seq, wide = qkv.shape
    width = wide // 3
    return pl.pallas_call(
        lambda *refs: attn_bwd_kernel(math.log(seq), heads, *refs),
        out_shape=jax.ShapeDtypeStruct((count, seq, wide), BF16),
        grid_spec=pltpu.PrefetchScalarGridSpec(
            num_scalar_prefetch=1,
            grid=(count,),
            in_specs=[
                pl.BlockSpec((None, seq, wide), lambda b, lens: (b, 0, 0)),
                pl.BlockSpec((None, seq, width), lambda b, lens: (b, 0, 0)),
            ],
            out_specs=pl.BlockSpec((None, seq, wide), lambda b, lens: (b, 0, 0)),
            scratch_shapes=[pltpu.VMEM((seq, width), F32), pltpu.VMEM((seq, width), F32)],
        ),
        cost_estimate=pl.CostEstimate(
            flops=20 * count * seq * seq * width, bytes_accessed=14 * count * seq * width, transcendentals=count * seq * seq * heads
        ),
        name="attn_bwd",
    )(lens, qkv, grad)


def swap(value, axis):
    return lax.ppermute(value, axis, [(0, 1), (1, 0)])


def shift_x(value, step):
    size = lax.axis_size("x")
    return lax.ppermute(value, "x", [((i + step) % size, i) for i in range(size)])


def relative_ranks():
    size = lax.axis_size("x")
    return [(dx, dc, dy) for dx in range(size) for dc in range(2) for dy in range(2)]


def plane_gather(own):
    size = lax.axis_size("x")
    half = own.shape[0] // 2
    by_place = {(0, 0): own}
    if size == 2:
        over_x = shift_x(own, 1)
        over_y = swap(own, "y")
        by_place[1, 0] = over_x
        by_place[0, 1] = over_y
        first = shift_x(over_y[:half], 1)
        second = swap(over_x[half:], "y")
        by_place[1, 1] = jnp.concatenate([first, second], axis=0)
    else:
        for dx in range(1, size):
            by_place[dx, 0] = shift_x(own, dx)
        for dx in range(size):
            by_place[dx, 1] = swap(by_place[dx, 0], "y")
    other = {place: swap(value, "c") for place, value in by_place.items()}
    return [(by_place, other)[dc][dx, dy] for dx, dc, dy in relative_ranks()]


def plane_scatter(parts):
    size = parts.shape[0]
    core = parts[:, 0].astype(F32) + swap(parts[:, 1], "c").astype(F32)
    if size == 2:
        half = core.shape[2] // 2
        low = core.astype(BF16)
        from_x = shift_x(low[1, :, :half], 1).astype(F32)
        from_y = swap(low[:, 1, half:], "y").astype(F32)
        top = core[0, :, :half] + from_x
        bottom = core[:, 0, half:] + from_y
        top_sum = top[0] + swap(top[1].astype(BF16), "y").astype(F32)
        bottom_sum = bottom[0] + shift_x(bottom[1].astype(BF16), 1).astype(F32)
        return jnp.concatenate([top_sum, bottom_sum], axis=0)
    core = core[:, 0] + swap(core[:, 1].astype(BF16), "y").astype(F32)
    total = core[0]
    for dx in range(1, size):
        total = total + shift_x(core[size - dx].astype(BF16), dx).astype(F32)
    return total


def all_to_all(value):
    return lax.all_to_all(value, PLANE, split_axis=0, concat_axis=0, tiled=True)


def local(
    tokens,
    w_query,
    w_key,
    w_value,
    w_out,
    gain_attn,
    w_gate,
    w_up,
    w_down,
    gain_ffn,
    counts,
    cotangent,
):
    size_x, size_z = lax.axis_size("x"), lax.axis_size("z")
    seq_ranks = 2 * size_x
    ranks = 2 * seq_ranks
    at_x, at_c, at_y = lax.axis_index("x"), lax.axis_index("c"), lax.axis_index("y")
    mine = tokens[0]
    row_count, width = mine.shape
    rows = w_query.shape[0]
    head_width = width // ranks
    heads = HEADS // ranks
    ff_rows = w_down.shape[0]
    ff_width = size_z * ff_rows
    relative = relative_ranks()
    places = [(lax.rem(at_x + dx, size_x) * 2 + (at_c ^ dc), at_y ^ dy) for dx, dc, dy in relative]

    pack_width = 1
    while pack_width < 3 * head_width + 2:
        pack_width *= 2
    gains = jnp.stack([gain_attn, gain_ffn], axis=1)
    first = jnp.concatenate(
        [w.reshape(rows, ranks, head_width) for w in (w_query, w_key, w_value)]
        + [
            jnp.broadcast_to(
                jnp.pad(gains, ((0, 0), (0, pack_width - 3 * head_width - 2)))[:, None, :],
                (rows, ranks, pack_width - 3 * head_width),
            )
        ],
        axis=2,
    ).transpose(1, 0, 2)
    first = all_to_all(first).reshape(ranks * rows, pack_width)
    pieces = width // pack_width
    out_pack = w_out.reshape(rows, pieces, pack_width).transpose(1, 0, 2).reshape(pieces * rows, pack_width)
    attn_pack = lax.all_gather(jnp.concatenate([first, out_pack], axis=0), "z", axis=0, tiled=False)

    def ff_columns(weight):
        return (
            weight.reshape(rows, seq_ranks, size_z, 2, ff_rows)
            .transpose(1, 3, 0, 2, 4)
            .reshape(ranks, rows, ff_width)
        )

    second = all_to_all(jnp.concatenate([ff_columns(w_gate), ff_columns(w_up)], axis=2)).reshape(
        ranks * rows, 2 * ff_width
    )
    down_pieces = width // (2 * ff_width)
    down_pack = (
        w_down.reshape(ff_rows, down_pieces, 2 * ff_width)
        .transpose(1, 0, 2)
        .reshape(down_pieces * ff_rows, 2 * ff_width)
    )
    ffn_pack = lax.all_gather(jnp.concatenate([second, down_pack], axis=0), "z", axis=0, tiled=False)

    def by_rows(pack):
        return (
            pack[:, : ranks * rows]
            .reshape(size_z, seq_ranks, 2, rows, pack.shape[-1])
            .transpose(1, 0, 2, 3, 4)
            .reshape(width, pack.shape[-1])
        )

    attn_full = by_rows(attn_pack)
    w_qkv = attn_full[:, : 3 * head_width]
    gain_one = attn_full[:, 3 * head_width].astype(F32)
    gain_two = attn_full[:, 3 * head_width + 1].astype(F32)
    out_block = (
        attn_pack[:, ranks * rows :]
        .reshape(size_z, pieces, rows, pack_width)
        .transpose(0, 2, 1, 3)
        .reshape(size_z, rows, width)
    )
    w_out_full = jnp.zeros((seq_ranks, size_z, 2, rows, width), BF16)
    for block, (s, y) in zip(plane_gather(out_block), places):
        w_out_full = lax.dynamic_update_slice(w_out_full, block[None, :, None], (s, 0, y, 0, 0))
    w_out_full = w_out_full.reshape(width, width)

    all_tokens = jnp.zeros((2, seq_ranks, row_count, width), BF16)
    for block, (s, y) in zip(plane_gather(mine), places):
        all_tokens = lax.dynamic_update_slice(all_tokens, block[None, None], (y, s, 0, 0))
    all_tokens = all_tokens.reshape(ranks * row_count, width).astype(F32)
    my_length = jnp.sum(counts, axis=1)
    other_length = swap(my_length, "y")
    lens = jnp.where(at_y == 0, jnp.concatenate([my_length, other_length]), jnp.concatenate([other_length, my_length]))

    normed_attn = (all_tokens * rms_scale(all_tokens) * gain_one).astype(BF16)
    qkv = dot(normed_attn, w_qkv).astype(BF16)
    qkv = qkv.reshape(2, seq_ranks * row_count, 3 * head_width)
    attended = attn_fwd(lens, qkv, heads)
    attended = (
        attended.reshape(2, seq_ranks, row_count, head_width)
        .transpose(1, 0, 2, 3)
        .reshape(ranks, row_count, head_width)
    )
    attended = all_to_all(attended).transpose(1, 0, 2).reshape(row_count, width)

    source = mine.astype(F32)
    resid = source + dot(attended, w_out_full)
    normed_ffn = (resid * rms_scale(resid) * gain_two).astype(BF16)

    cot_all = jnp.concatenate(plane_gather(cotangent[0]), axis=0)
    normed_all = jnp.concatenate(plane_gather(normed_ffn), axis=0)
    ffn_full = by_rows(ffn_pack)
    w_gate_mine, w_up_mine = ffn_full[:, :ff_width], ffn_full[:, ff_width:]
    w_down_mine = (
        ffn_pack[:, ranks * rows :]
        .reshape(size_z, down_pieces, ff_rows, 2 * ff_width)
        .transpose(0, 2, 1, 3)
        .reshape(ff_width, width)
    )
    gate = dot(normed_all, w_gate_mine)
    up_proj = dot(normed_all, w_up_mine)
    gate_sigma = jax.nn.sigmoid(gate)
    hidden = (gate * gate_sigma * up_proj).astype(BF16)
    grad_hidden = dot_nt(cot_all, w_down_mine)
    grad_gate = (
        grad_hidden * up_proj * (gate_sigma + gate * gate_sigma * (1.0 - gate_sigma))
    ).astype(BF16)
    grad_up = (grad_hidden * gate * gate_sigma).astype(BF16)
    grad_both = jnp.concatenate([grad_gate, grad_up], axis=1)
    in_blocks = (size_x, 2, 2, row_count, width)
    grad_normed_ffn = plane_scatter(dot_nt(grad_both, ffn_full).astype(BF16).reshape(in_blocks))
    ffn_out = plane_scatter(dot(hidden, w_down_mine).astype(BF16).reshape(in_blocks))
    block_output = (resid + ffn_out).astype(BF16)

    def by_z(grad):
        return (
            grad.astype(BF16)
            .reshape(seq_ranks, size_z, 2, rows, grad.shape[-1])
            .transpose(1, 0, 2, 3, 4)
            .reshape(size_z, ranks * rows, grad.shape[-1])
        )

    grad_down = (
        dot_tn(hidden, cot_all)
        .astype(BF16)
        .reshape(size_z, ff_rows, down_pieces, 2 * ff_width)
        .transpose(0, 2, 1, 3)
        .reshape(size_z, down_pieces * ff_rows, 2 * ff_width)
    )
    ffn_grads = lax.psum_scatter(
        jnp.concatenate([by_z(dot_tn(normed_all, grad_both)), grad_down], axis=1),
        "z",
        scatter_dimension=0,
        tiled=True,
    )[0]
    grad_w_down = (
        ffn_grads[ranks * rows :]
        .reshape(down_pieces, ff_rows, 2 * ff_width)
        .transpose(1, 0, 2)
        .reshape(ff_rows, width)
        .astype(F32)
    )
    ffn_columns = all_to_all(ffn_grads[: ranks * rows].reshape(ranks, rows, 2 * ff_width))
    ffn_columns = (
        ffn_columns.reshape(seq_ranks, 2, rows, 2, size_z, ff_rows)
        .transpose(3, 2, 0, 4, 1, 5)
        .reshape(2, rows, ranks * ff_width)
        .astype(F32)
    )

    cot_mine = cotangent[0].astype(F32)
    grad_norm_two, grad_gain_ffn = norm_back(grad_normed_ffn, resid, gain_two)
    grad_resid = cot_mine + grad_norm_two
    resid_low = grad_resid.astype(BF16)
    grad_attended = dot_nt(resid_low, w_out_full).astype(BF16)
    grad_attended = all_to_all(grad_attended.reshape(row_count, ranks, head_width).transpose(1, 0, 2))
    grad_attended = (
        grad_attended.reshape(seq_ranks, 2, row_count, head_width)
        .transpose(1, 0, 2, 3)
        .reshape(2, seq_ranks * row_count, head_width)
    )
    grad_qkv = attn_bwd(lens, qkv, grad_attended, heads)
    by_block = grad_qkv.reshape(2, seq_ranks, row_count, 3 * head_width)
    in_order = jnp.concatenate(
        [
            lax.dynamic_slice(by_block, (y, s, 0, 0), (1, 1, row_count, 3 * head_width))[0, 0]
            for s, y in places
        ],
        axis=0,
    )
    grad_normed_attn = plane_scatter(dot_nt(in_order, w_qkv).astype(BF16).reshape(in_blocks))
    grad_norm_one, grad_gain_attn = norm_back(grad_normed_attn, source, gain_one)
    input_grad = grad_resid + grad_norm_one

    grad_out = dot_tn(attended, resid_low).astype(BF16).reshape(seq_ranks, size_z, 2, rows, width)
    grad_out = jnp.stack(
        [
            lax.dynamic_slice(grad_out, (s, 0, y, 0, 0), (1, size_z, 1, rows, width)).reshape(size_z * rows, width)
            for s, y in places
        ]
    ).reshape(size_x, 2, 2, size_z * rows, width)
    grad_out = plane_scatter(grad_out).astype(BF16).reshape(size_z, rows, width)
    w_grads = dot_tn(normed_attn, grad_qkv.reshape(ranks * row_count, 3 * head_width))
    w_grads = by_z(w_grads)
    packed = jnp.concatenate(
        [w_grads[:, :, i * head_width : (i + 1) * head_width] for i in range(3)]
        + [grad_out[:, :, i * head_width : (i + 1) * head_width] for i in range(ranks)],
        axis=1,
    )
    packed = lax.psum_scatter(packed, "z", scatter_dimension=0, tiled=True)[0]
    cut = 3 * ranks * rows
    grad_w_out = (
        packed[cut:].reshape(ranks, rows, head_width).transpose(1, 0, 2).reshape(rows, width).astype(F32)
    )
    columns = all_to_all(packed[:cut].reshape(3, ranks, rows, head_width).transpose(1, 0, 2, 3))
    columns = columns.transpose(1, 2, 0, 3).reshape(3, rows, width).astype(F32)

    gain_grads = jnp.stack([grad_gain_attn, grad_gain_ffn])
    gain_grads = gain_grads.reshape(2, seq_ranks, size_z, 2, rows).transpose(1, 3, 0, 2, 4)
    gain_grads = jnp.sum(all_to_all(gain_grads.reshape(ranks, 2, size_z, rows)), axis=0)
    gain_grads = lax.all_to_all(gain_grads.transpose(1, 0, 2), "z", split_axis=0, concat_axis=0, tiled=True)
    gain_grads = jnp.sum(gain_grads, axis=0)
    return (
        block_output[None],
        input_grad[None],
        columns[0],
        columns[1],
        columns[2],
        grad_w_out,
        gain_grads[0],
        ffn_columns[0],
        ffn_columns[1],
        grad_w_down,
        gain_grads[1],
    )


def solution(mesh):
    seq, batch = mesh.shape["seq"], mesh.shape["batch"]
    fine = Mesh(mesh.devices.reshape(seq // 2, 2, batch // 2, 2), ("x", "c", "z", "y"))
    token_spec = P(("z", "y"), ("x", "c"), None)
    row_spec = P(("x", "c", "z", "y"), None)
    gain_spec = P(("x", "c", "z", "y"))
    in_specs = (
        (token_spec,)
        + (row_spec,) * 4
        + (gain_spec,)
        + (row_spec,) * 3
        + (gain_spec, P(("z", "y"), None), token_spec)
    )
    out_specs = (
        (token_spec,) * 2
        + (row_spec,) * 4
        + (gain_spec,)
        + (row_spec,) * 3
        + (gain_spec,)
    )
    return jax.shard_map(local, mesh=fine, in_specs=in_specs, out_specs=out_specs, check_vma=False)
```

```python
import math

import jax
import jax.numpy as jnp
from jax import lax
from jax.experimental import pallas as pl
from jax.experimental.pallas import tpu as pltpu
from jax.sharding import Mesh
from jax.sharding import PartitionSpec as P

HEADS = 16
EPSILON = 1e-05
TILE = 256
PLANE = ("x", "c", "y")
F32 = jnp.float32
BF16 = jnp.bfloat16


def rms_scale(source):
    return lax.rsqrt(jnp.mean(source * source, axis=-1, keepdims=True) + EPSILON)


def norm_back(incoming, source, gain_full):
    inverse = rms_scale(source)
    scaled = incoming * gain_full
    grad_source = inverse * (
        scaled - source * (inverse * inverse) * jnp.mean(scaled * source, axis=-1, keepdims=True)
    )
    grad_gain = jnp.sum(incoming * source * inverse, axis=0)
    return (grad_source, grad_gain)


def dot(left, right):
    return jnp.dot(left, right, preferred_element_type=F32)


def dot_nt(left, right):
    return lax.dot_general(left, right, (((1,), (1,)), ((), ())), preferred_element_type=F32)


def dot_tn(left, right):
    return lax.dot_general(left, right, (((0,), (0,)), ((), ())), preferred_element_type=F32)


def lane_masks(width, count):
    lane = lax.broadcasted_iota(jnp.int32, (1, width), 1)
    return [(lane // (width // count)) == h for h in range(count)]


def spread(block, masks):
    zero = jnp.zeros_like(block)
    return jnp.concatenate([jnp.where(m, block, zero) for m in masks], axis=0)


def gather_heads(stacked, masks):
    rows = stacked.shape[0] // len(masks)
    total = jnp.where(masks[0], stacked[:rows], 0.0)
    for h in range(1, len(masks)):
        total = jnp.where(masks[h], stacked[h * rows : (h + 1) * rows], total)
    return total


def rows_of(ref, tile):
    return ref.at[tile] if len(ref.shape) == 3 else ref.at[tile * TILE : (tile + 1) * TILE]


def attn_fwd_kernel(offset, heads, lens_ref, qkv_ref, out_ref):
    length = lens_ref[pl.program_id(0)]
    seq, width = qkv_ref.shape[0], qkv_ref.shape[1] // 3
    scale = (width // heads) ** -0.5
    masks = lane_masks(width, heads)
    for i in range(seq // TILE):
        q = spread(qkv_ref[i * TILE : (i + 1) * TILE, :width] * jnp.asarray(scale, BF16), masks)
        acc = jnp.zeros((heads * TILE, width), F32)
        for j in range(i + 1):
            k = qkv_ref[j * TILE : (j + 1) * TILE, width : 2 * width]
            v = qkv_ref[j * TILE : (j + 1) * TILE, 2 * width :]
            scores = dot_nt(q, k)
            gates = 1.0 / (1.0 + jnp.exp(offset - scores))
            key = lax.broadcasted_iota(jnp.int32, (heads * TILE, TILE), 1)
            allowed = key < length - j * TILE
            if j == i:
                row = lax.broadcasted_iota(jnp.int32, (heads * TILE, TILE), 0) % TILE
                allowed = allowed & (key <= row)
            probs = jnp.where(allowed, gates, 0.0).astype(BF16)
            acc = acc + dot(probs, v)
        rows_of(out_ref, i)[...] = gather_heads(acc, masks).astype(BF16)


def attn_bwd_kernel(offset, heads, lens_ref, qkv_ref, grad_ref, out_ref, dk_ref, dv_ref):
    length = lens_ref[pl.program_id(0)]
    seq, width = qkv_ref.shape[0], qkv_ref.shape[1] // 3
    scale = (width // heads) ** -0.5
    masks = lane_masks(width, heads)
    steps = seq // TILE
    for i in range(steps):
        rows = slice(i * TILE, (i + 1) * TILE)
        q = spread(qkv_ref[rows, :width] * jnp.asarray(scale, BF16), masks)
        grad = spread(rows_of(grad_ref, i)[...], masks)
        dq = jnp.zeros((heads * TILE, width), F32)
        for j in range(i + 1):
            cols = slice(j * TILE, (j + 1) * TILE)
            k = qkv_ref[cols, width : 2 * width]
            v = qkv_ref[cols, 2 * width :]
            scores = dot_nt(k, q)
            gates = 1.0 / (1.0 + jnp.exp(offset - scores))
            key = lax.broadcasted_iota(jnp.int32, (TILE, heads * TILE), 0)
            allowed = key < length - j * TILE
            if j == i:
                row = lax.broadcasted_iota(jnp.int32, (TILE, heads * TILE), 1) % TILE
                allowed = allowed & (key <= row)
            gates = jnp.where(allowed, gates, 0.0)
            grad_scores = (dot_nt(v, grad) * gates * (1.0 - gates)).astype(BF16)
            dv = dot(gates.astype(BF16), grad)
            dk = dot(grad_scores, q)
            dq = dq + dot_tn(grad_scores, k)
            if i == j:
                dv_ref[cols, :] = dv
                dk_ref[cols, :] = dk
            else:
                dv_ref[cols, :] += dv
                dk_ref[cols, :] += dk
        out_ref[rows, :width] = (gather_heads(dq, masks) * scale).astype(BF16)
    out_ref[:, width : 2 * width] = dk_ref[...].astype(BF16)
    out_ref[:, 2 * width :] = dv_ref[...].astype(BF16)


def attn_fwd(lens, qkv, heads, block=None):
    count, seq, wide = qkv.shape
    width = wide // 3
    out = jax.ShapeDtypeStruct((count, seq, width), BF16)
    out_spec = pl.BlockSpec((None, seq, width), lambda b, lens: (b, 0, 0))
    if block:
        out = jax.ShapeDtypeStruct((seq // block, count, block, width), BF16)
        out_spec = pl.BlockSpec((seq // block, None, block, width), lambda b, lens: (0, b, 0, 0))
    return pl.pallas_call(
        lambda *refs: attn_fwd_kernel(math.log(seq), heads, *refs),
        out_shape=out,
        grid_spec=pltpu.PrefetchScalarGridSpec(
            num_scalar_prefetch=1,
            grid=(count,),
            in_specs=[pl.BlockSpec((None, seq, wide), lambda b, lens: (b, 0, 0))],
            out_specs=out_spec,
        ),
        cost_estimate=pl.CostEstimate(
            flops=8 * count * seq * seq * width, bytes_accessed=8 * count * seq * width, transcendentals=count * seq * seq * heads
        ),
        name="attn_fwd",
    )(lens, qkv)


def attn_bwd(lens, qkv, grad, heads, block=None):
    count, seq, wide = qkv.shape
    width = wide // 3
    grad_spec = pl.BlockSpec((None, seq, width), lambda b, lens: (b, 0, 0))
    if block:
        grad_spec = pl.BlockSpec((seq // block, None, block, width), lambda b, lens: (0, b, 0, 0))
    return pl.pallas_call(
        lambda *refs: attn_bwd_kernel(math.log(seq), heads, *refs),
        out_shape=jax.ShapeDtypeStruct((count, seq, wide), BF16),
        grid_spec=pltpu.PrefetchScalarGridSpec(
            num_scalar_prefetch=1,
            grid=(count,),
            in_specs=[
                pl.BlockSpec((None, seq, wide), lambda b, lens: (b, 0, 0)),
                grad_spec,
            ],
            out_specs=pl.BlockSpec((None, seq, wide), lambda b, lens: (b, 0, 0)),
            scratch_shapes=[pltpu.VMEM((seq, width), F32), pltpu.VMEM((seq, width), F32)],
        ),
        cost_estimate=pl.CostEstimate(
            flops=20 * count * seq * seq * width, bytes_accessed=14 * count * seq * width, transcendentals=count * seq * seq * heads
        ),
        name="attn_bwd",
    )(lens, qkv, grad)


def swap(value, axis):
    return lax.ppermute(value, axis, [(0, 1), (1, 0)])


def shift_x(value, step):
    size = lax.axis_size("x")
    return lax.ppermute(value, "x", [((i + step) % size, i) for i in range(size)])


def relative_ranks():
    size = lax.axis_size("x")
    return [(dx, dc, dy) for dx in range(size) for dc in range(2) for dy in range(2)]


def plane_gather(own):
    size = lax.axis_size("x")
    half = own.shape[0] // 2
    by_place = {(0, 0): own}
    if size == 2:
        over_x = shift_x(own, 1)
        over_y = swap(own, "y")
        by_place[1, 0] = over_x
        by_place[0, 1] = over_y
        first = shift_x(over_y[:half], 1)
        second = swap(over_x[half:], "y")
        by_place[1, 1] = jnp.concatenate([first, second], axis=0)
    else:
        for dx in range(1, size):
            by_place[dx, 0] = shift_x(own, dx)
        for dx in range(size):
            by_place[dx, 1] = swap(by_place[dx, 0], "y")
    other = {place: swap(value, "c") for place, value in by_place.items()}
    return [(by_place, other)[dc][dx, dy] for dx, dc, dy in relative_ranks()]


def plane_scatter(parts):
    size = parts.shape[0]
    core = parts[:, 0].astype(F32) + swap(parts[:, 1], "c").astype(F32)
    if size == 2:
        half = core.shape[2] // 2
        low = core.astype(BF16)
        from_x = shift_x(low[1, :, :half], 1).astype(F32)
        from_y = swap(low[:, 1, half:], "y").astype(F32)
        top = core[0, :, :half] + from_x
        bottom = core[:, 0, half:] + from_y
        top_sum = top[0] + swap(top[1].astype(BF16), "y").astype(F32)
        bottom_sum = bottom[0] + shift_x(bottom[1].astype(BF16), 1).astype(F32)
        return jnp.concatenate([top_sum, bottom_sum], axis=0)
    core = core[:, 0] + swap(core[:, 1].astype(BF16), "y").astype(F32)
    total = core[0]
    for dx in range(1, size):
        total = total + shift_x(core[size - dx].astype(BF16), dx).astype(F32)
    return total


def all_to_all(value):
    return lax.all_to_all(value, PLANE, split_axis=0, concat_axis=0, tiled=True)


def local_any(
    tokens,
    w_query,
    w_key,
    w_value,
    w_out,
    gain_attn,
    w_gate,
    w_up,
    w_down,
    gain_ffn,
    counts,
    cotangent,
):
    size_x, size_z = lax.axis_size("x"), lax.axis_size("z")
    seq_ranks = 2 * size_x
    ranks = 2 * seq_ranks
    at_x, at_c, at_y = lax.axis_index("x"), lax.axis_index("c"), lax.axis_index("y")
    mine = tokens[0]
    row_count, width = mine.shape
    rows = w_query.shape[0]
    head_width = width // ranks
    heads = HEADS // ranks
    ff_rows = w_down.shape[0]
    ff_width = size_z * ff_rows
    relative = relative_ranks()
    places = [(lax.rem(at_x + dx, size_x) * 2 + (at_c ^ dc), at_y ^ dy) for dx, dc, dy in relative]

    pack_width = 1
    while pack_width < 3 * head_width + 2:
        pack_width *= 2
    gains = jnp.stack([gain_attn, gain_ffn], axis=1)
    first = jnp.concatenate(
        [w.reshape(rows, ranks, head_width) for w in (w_query, w_key, w_value)]
        + [
            jnp.broadcast_to(
                jnp.pad(gains, ((0, 0), (0, pack_width - 3 * head_width - 2)))[:, None, :],
                (rows, ranks, pack_width - 3 * head_width),
            )
        ],
        axis=2,
    ).transpose(1, 0, 2)
    first = all_to_all(first).reshape(ranks * rows, pack_width)
    pieces = width // pack_width
    out_pack = w_out.reshape(rows, pieces, pack_width).transpose(1, 0, 2).reshape(pieces * rows, pack_width)
    attn_pack = lax.all_gather(jnp.concatenate([first, out_pack], axis=0), "z", axis=0, tiled=False)

    def ff_columns(weight):
        return (
            weight.reshape(rows, seq_ranks, size_z, 2, ff_rows)
            .transpose(1, 3, 0, 2, 4)
            .reshape(ranks, rows, ff_width)
        )

    second = all_to_all(jnp.concatenate([ff_columns(w_gate), ff_columns(w_up)], axis=2)).reshape(
        ranks * rows, 2 * ff_width
    )
    down_pieces = width // (2 * ff_width)
    down_pack = (
        w_down.reshape(ff_rows, down_pieces, 2 * ff_width)
        .transpose(1, 0, 2)
        .reshape(down_pieces * ff_rows, 2 * ff_width)
    )
    ffn_pack = lax.all_gather(jnp.concatenate([second, down_pack], axis=0), "z", axis=0, tiled=False)

    def by_rows(pack):
        return (
            pack[:, : ranks * rows]
            .reshape(size_z, seq_ranks, 2, rows, pack.shape[-1])
            .transpose(1, 0, 2, 3, 4)
            .reshape(width, pack.shape[-1])
        )

    attn_full = by_rows(attn_pack)
    w_qkv = attn_full[:, : 3 * head_width]
    gain_one = attn_full[:, 3 * head_width].astype(F32)
    gain_two = attn_full[:, 3 * head_width + 1].astype(F32)
    out_block = (
        attn_pack[:, ranks * rows :]
        .reshape(size_z, pieces, rows, pack_width)
        .transpose(0, 2, 1, 3)
        .reshape(size_z, rows, width)
    )
    w_out_full = jnp.zeros((seq_ranks, size_z, 2, rows, width), BF16)
    for block, (s, y) in zip(plane_gather(out_block), places):
        w_out_full = lax.dynamic_update_slice(w_out_full, block[None, :, None], (s, 0, y, 0, 0))
    w_out_full = w_out_full.reshape(width, width)

    all_tokens = jnp.zeros((2, seq_ranks, row_count, width), BF16)
    for block, (s, y) in zip(plane_gather(mine), places):
        all_tokens = lax.dynamic_update_slice(all_tokens, block[None, None], (y, s, 0, 0))
    all_tokens = all_tokens.reshape(ranks * row_count, width).astype(F32)
    my_length = jnp.sum(counts, axis=1)
    other_length = swap(my_length, "y")
    lens = jnp.where(at_y == 0, jnp.concatenate([my_length, other_length]), jnp.concatenate([other_length, my_length]))

    normed_attn = (all_tokens * rms_scale(all_tokens) * gain_one).astype(BF16)
    qkv = dot(normed_attn, w_qkv).astype(BF16)
    qkv = qkv.reshape(2, seq_ranks * row_count, 3 * head_width)
    attended = attn_fwd(lens, qkv, heads)
    attended = (
        attended.reshape(2, seq_ranks, row_count, head_width)
        .transpose(1, 0, 2, 3)
        .reshape(ranks, row_count, head_width)
    )
    attended = all_to_all(attended).transpose(1, 0, 2).reshape(row_count, width)

    source = mine.astype(F32)
    resid = source + dot(attended, w_out_full)
    normed_ffn = (resid * rms_scale(resid) * gain_two).astype(BF16)

    cot_all = jnp.concatenate(plane_gather(cotangent[0]), axis=0)
    normed_all = jnp.concatenate(plane_gather(normed_ffn), axis=0)
    ffn_full = by_rows(ffn_pack)
    w_gate_mine, w_up_mine = ffn_full[:, :ff_width], ffn_full[:, ff_width:]
    w_down_mine = (
        ffn_pack[:, ranks * rows :]
        .reshape(size_z, down_pieces, ff_rows, 2 * ff_width)
        .transpose(0, 2, 1, 3)
        .reshape(ff_width, width)
    )
    gate = dot(normed_all, w_gate_mine)
    up_proj = dot(normed_all, w_up_mine)
    gate_sigma = jax.nn.sigmoid(gate)
    hidden = (gate * gate_sigma * up_proj).astype(BF16)
    grad_hidden = dot_nt(cot_all, w_down_mine)
    grad_gate = (
        grad_hidden * up_proj * (gate_sigma + gate * gate_sigma * (1.0 - gate_sigma))
    ).astype(BF16)
    grad_up = (grad_hidden * gate * gate_sigma).astype(BF16)
    grad_both = jnp.concatenate([grad_gate, grad_up], axis=1)
    in_blocks = (size_x, 2, 2, row_count, width)
    grad_normed_ffn = plane_scatter(dot_nt(grad_both, ffn_full).astype(BF16).reshape(in_blocks))
    ffn_out = plane_scatter(dot(hidden, w_down_mine).astype(BF16).reshape(in_blocks))
    block_output = (resid + ffn_out).astype(BF16)

    def by_z(grad):
        return (
            grad.astype(BF16)
            .reshape(seq_ranks, size_z, 2, rows, grad.shape[-1])
            .transpose(1, 0, 2, 3, 4)
            .reshape(size_z, ranks * rows, grad.shape[-1])
        )

    grad_down = (
        dot_tn(hidden, cot_all)
        .astype(BF16)
        .reshape(size_z, ff_rows, down_pieces, 2 * ff_width)
        .transpose(0, 2, 1, 3)
        .reshape(size_z, down_pieces * ff_rows, 2 * ff_width)
    )
    ffn_grads = lax.psum_scatter(
        jnp.concatenate([by_z(dot_tn(normed_all, grad_both)), grad_down], axis=1),
        "z",
        scatter_dimension=0,
        tiled=True,
    )[0]
    grad_w_down = (
        ffn_grads[ranks * rows :]
        .reshape(down_pieces, ff_rows, 2 * ff_width)
        .transpose(1, 0, 2)
        .reshape(ff_rows, width)
        .astype(F32)
    )
    ffn_columns = all_to_all(ffn_grads[: ranks * rows].reshape(ranks, rows, 2 * ff_width))
    ffn_columns = (
        ffn_columns.reshape(seq_ranks, 2, rows, 2, size_z, ff_rows)
        .transpose(3, 2, 0, 4, 1, 5)
        .reshape(2, rows, ranks * ff_width)
        .astype(F32)
    )

    cot_mine = cotangent[0].astype(F32)
    grad_norm_two, grad_gain_ffn = norm_back(grad_normed_ffn, resid, gain_two)
    grad_resid = cot_mine + grad_norm_two
    resid_low = grad_resid.astype(BF16)
    grad_attended = dot_nt(resid_low, w_out_full).astype(BF16)
    grad_attended = all_to_all(grad_attended.reshape(row_count, ranks, head_width).transpose(1, 0, 2))
    grad_attended = (
        grad_attended.reshape(seq_ranks, 2, row_count, head_width)
        .transpose(1, 0, 2, 3)
        .reshape(2, seq_ranks * row_count, head_width)
    )
    grad_qkv = attn_bwd(lens, qkv, grad_attended, heads)
    by_block = grad_qkv.reshape(2, seq_ranks, row_count, 3 * head_width)
    in_order = jnp.concatenate(
        [
            lax.dynamic_slice(by_block, (y, s, 0, 0), (1, 1, row_count, 3 * head_width))[0, 0]
            for s, y in places
        ],
        axis=0,
    )
    grad_normed_attn = plane_scatter(dot_nt(in_order, w_qkv).astype(BF16).reshape(in_blocks))
    grad_norm_one, grad_gain_attn = norm_back(grad_normed_attn, source, gain_one)
    input_grad = grad_resid + grad_norm_one

    grad_out = dot_tn(attended, resid_low).astype(BF16).reshape(seq_ranks, size_z, 2, rows, width)
    grad_out = jnp.stack(
        [
            lax.dynamic_slice(grad_out, (s, 0, y, 0, 0), (1, size_z, 1, rows, width)).reshape(size_z * rows, width)
            for s, y in places
        ]
    ).reshape(size_x, 2, 2, size_z * rows, width)
    grad_out = plane_scatter(grad_out).astype(BF16).reshape(size_z, rows, width)
    w_grads = dot_tn(normed_attn, grad_qkv.reshape(ranks * row_count, 3 * head_width))
    w_grads = by_z(w_grads)
    packed = jnp.concatenate(
        [w_grads[:, :, i * head_width : (i + 1) * head_width] for i in range(3)]
        + [grad_out[:, :, i * head_width : (i + 1) * head_width] for i in range(ranks)],
        axis=1,
    )
    packed = lax.psum_scatter(packed, "z", scatter_dimension=0, tiled=True)[0]
    cut = 3 * ranks * rows
    grad_w_out = (
        packed[cut:].reshape(ranks, rows, head_width).transpose(1, 0, 2).reshape(rows, width).astype(F32)
    )
    columns = all_to_all(packed[:cut].reshape(3, ranks, rows, head_width).transpose(1, 0, 2, 3))
    columns = columns.transpose(1, 2, 0, 3).reshape(3, rows, width).astype(F32)

    gain_grads = jnp.stack([grad_gain_attn, grad_gain_ffn])
    gain_grads = gain_grads.reshape(2, seq_ranks, size_z, 2, rows).transpose(1, 3, 0, 2, 4)
    gain_grads = jnp.sum(all_to_all(gain_grads.reshape(ranks, 2, size_z, rows)), axis=0)
    gain_grads = lax.all_to_all(gain_grads.transpose(1, 0, 2), "z", split_axis=0, concat_axis=0, tiled=True)
    gain_grads = jnp.sum(gain_grads, axis=0)
    return (
        block_output[None],
        input_grad[None],
        columns[0],
        columns[1],
        columns[2],
        grad_w_out,
        gain_grads[0],
        ffn_columns[0],
        ffn_columns[1],
        grad_w_down,
        gain_grads[1],
    )


SENT = [(1, dx, dy) for dx in range(2) for dy in range(2)]
KEPT = [(0, dx, dy) for dx in range(2) for dy in range(2)]
ANY = pl.BlockSpec(memory_space=pl.ANY)


def fits(fine):
    shape = fine.shape
    return shape["x"] == 2 and shape["z"] == 4 and HEADS == 2 * 2 * shape["x"] * shape["y"]


def shape_of(shape, dtype=BF16):
    return jax.ShapeDtypeStruct(tuple(shape), dtype)


def whole(kernel, outs, ins, flops=0):
    size = sum(math.prod(a.shape) * a.dtype.itemsize for a in (*outs, *ins))
    return pl.pallas_call(
        kernel,
        out_shape=tuple(outs),
        in_specs=[pl.BlockSpec(memory_space=pltpu.VMEM)] * len(ins),
        out_specs=tuple(pl.BlockSpec(memory_space=pltpu.VMEM) for _ in outs),
        cost_estimate=pl.CostEstimate(flops=flops, bytes_accessed=size, transcendentals=0),
    )(*ins)


def scatter_z(sums):
    return lax.psum_scatter(sums, "z", scatter_dimension=0, tiled=True)[0]


def gather_parts(own):
    half = own.shape[0] // 2
    over_x = shift_x(own, 1)
    over_y = swap(own, "y")
    low = shift_x(over_y[:half], 1)
    high = swap(over_x[half:], "y")
    near = {(0, 0): [own], (0, 1): [over_y], (1, 0): [over_x], (1, 1): [low, high]}
    parts = {}
    for (dx, dy), pieces in near.items():
        parts[0, dx, dy] = pieces
        parts[1, dx, dy] = [swap(piece, "c") for piece in pieces]
    return parts


def flat(parts, order):
    return [piece for place in order for piece in parts[place]]


def layout(parts, order):
    return [len(parts[place]) for place in order]


def start_all(refs, counts, buffer, sem):
    at = 0
    for index, count in enumerate(counts):
        row = 0
        for ref in refs[at : at + count]:
            pltpu.make_async_copy(ref, buffer.at[index, row : row + ref.shape[0]], sem.at[index]).start()
            row += ref.shape[0]
        at += count


def wait_for(buffer, sem):
    pltpu.make_async_copy(buffer, buffer, sem).wait()


def pack_kernel(size_z, q, k, v, o, g, u, gains, first, second, out):
    ranks, rows, wide = first.shape
    width = (wide - gains.shape[1]) // 3
    ff = second.shape[2] // 2
    fine = ff // size_z
    for r in range(ranks):
        for n, w in enumerate((q, k, v)):
            first[r, :, n * width : (n + 1) * width] = w[:, r * width : (r + 1) * width]
        first[r, :, 3 * width :] = gains[...]
        s, y = r // 2, r % 2
        for n, w in enumerate((g, u)):
            for z in range(size_z):
                at = ((s * size_z + z) * 2 + y) * fine
                second[r, :, n * ff + z * fine : n * ff + (z + 1) * fine] = w[:, at : at + fine]
    for p in range(out.shape[0] // rows):
        out[p * rows : (p + 1) * rows, :] = o[:, p * wide : (p + 1) * wide]


def norm_qkv_kernel(counts, places, pack, *refs):
    n = sum(counts)
    pieces, (normed, qkv, w_all, gains, buffer, small, sem, out_sem, small_sem) = refs[:n], refs[n:]
    steps = len(counts)
    start_all(pieces, counts, buffer, sem)
    size_z, wide = pack.shape[0], w_all.shape[1]
    cell = 64
    seqs = w_all.shape[0] // (size_z * cell)
    lane = lax.broadcasted_iota(jnp.int32, (8, pack.shape[2] - wide), 1)
    row = lax.broadcasted_iota(jnp.int32, (8, pack.shape[2] - wide), 0)
    pick = jnp.where(lane == row, 1.0, 0.0).astype(BF16)
    for s in range(seqs):
        for z in range(size_z):
            at = (s * size_z + z) * cell
            w_all[at : at + cell, :] = pack[z, s * cell : (s + 1) * cell, :wide]
            gains[:, at : at + cell] = dot_nt(pick, pack[z, s * cell : (s + 1) * cell, wide:])

    @pl.loop(0, steps)
    def _(k):
        wait_for(buffer.at[k], sem.at[k])
        x = buffer[k].astype(F32)
        value = (x * rms_scale(x) * gains[0:1, :]).astype(BF16)
        buffer[k] = value
        small[k] = dot(value, w_all[...]).astype(BF16)
        pltpu.make_async_copy(buffer.at[k], normed.at[places[k]], out_sem.at[k]).start()
        pltpu.make_async_copy(small.at[k], qkv.at[places[k]], small_sem.at[k]).start()

    @pl.loop(0, steps)
    def _(k):
        wait_for(buffer.at[k], out_sem.at[k])
        wait_for(small.at[k], small_sem.at[k])


def norm_qkv(places, parts, pack, head_wide):
    order = SENT + KEPT
    counts = layout(parts, order)
    pieces = flat(parts, order)
    steps = len(order)
    row_count, width = parts[0, 0, 0][0].shape
    vmem = pl.BlockSpec(memory_space=pltpu.VMEM)
    return pl.pallas_call(
        lambda *refs: norm_qkv_kernel(counts, *refs),
        out_shape=(
            shape_of((steps, row_count, width)),
            shape_of((steps, row_count, head_wide)),
            shape_of((width, head_wide)),
            shape_of((8, width), F32),
        ),
        in_specs=[pl.BlockSpec(memory_space=pltpu.SMEM), vmem] + [ANY] * len(pieces),
        out_specs=(ANY, ANY, vmem, vmem),
        scratch_shapes=[
            pltpu.VMEM((steps, row_count, width), BF16),
            pltpu.VMEM((steps, row_count, head_wide), BF16),
            pltpu.SemaphoreType.DMA((steps,)),
            pltpu.SemaphoreType.DMA((steps,)),
            pltpu.SemaphoreType.DMA((steps,)),
        ],
        cost_estimate=pl.CostEstimate(
            flops=2 * steps * row_count * width * head_wide, bytes_accessed=6 * steps * row_count * width, transcendentals=0
        ),
        name="norm_qkv",
    )(places, pack, *pieces)


def out_block_kernel(first, rows, pack, out, sem):
    size_z, _, wide = pack.shape
    copies = []
    for z in range(size_z):
        for p in range(out.shape[1] // wide):
            source = pack.at[z, first + p * rows : first + (p + 1) * rows]
            target = out.at[z * rows : (z + 1) * rows, p * wide : (p + 1) * wide]
            copies.append(pltpu.make_async_copy(source, target, sem.at[z, p]))
    for copy in copies:
        copy.start()
    for copy in copies:
        copy.wait()


def out_block(pack, first, rows):
    size_z, total, wide = pack.shape
    pieces = (total - first) // rows
    return pl.pallas_call(
        lambda *refs: out_block_kernel(first, rows, *refs),
        out_shape=shape_of((size_z * rows, pieces * wide)),
        in_specs=[ANY],
        out_specs=pl.BlockSpec(memory_space=pltpu.VMEM),
        scratch_shapes=[pltpu.SemaphoreType.DMA((size_z, pieces))],
        cost_estimate=pl.CostEstimate(flops=0, bytes_accessed=4 * size_z * rows * pieces * wide, transcendentals=0),
        name="out_block",
    )(pack)


def out_weight_kernel(counts, cell, rows, seq_ref, y_ref, *refs):
    n = sum(counts)
    pieces, out = refs[:n], refs[n]
    at = 0
    for index, count in enumerate(counts):
        z = 0
        for ref in pieces[at : at + count]:
            for part in range(ref.shape[0] // rows):
                row = (seq_ref[index] * cell + z) * 2 * rows + y_ref[index] * rows
                out[pl.ds(pl.multiple_of(row, rows), rows), :] = ref[part * rows : (part + 1) * rows, :]
                z += 1
        at += count


def out_weight(seqs, ys, parts, size_z):
    order = SENT + KEPT
    counts = layout(parts, order)
    pieces = flat(parts, order)
    block, width = parts[0, 0, 0][0].shape
    full = pl.BlockSpec(memory_space=pltpu.VMEM)
    smem = pl.BlockSpec(memory_space=pltpu.SMEM)
    return pl.pallas_call(
        lambda *refs: out_weight_kernel(counts, size_z, block // size_z, *refs),
        out_shape=shape_of((len(order) * block, width)),
        in_specs=[smem, smem] + [full] * len(pieces),
        out_specs=full,
        cost_estimate=pl.CostEstimate(flops=0, bytes_accessed=4 * len(order) * block * width, transcendentals=0),
        name="out_weight",
    )(seqs, ys, *pieces)


def out_kernel(heads, tokens, w_out, gains, resid, normed, attended):
    ranks, _, width = heads.shape
    for r in range(ranks):
        attended[:, r * width : (r + 1) * width] = heads[r]
    total = tokens[...].astype(F32) + dot(attended[...], w_out[...])
    resid[...] = total
    normed[...] = (total * rms_scale(total) * gains[1:2, :]).astype(BF16)


def ffn_kernel(counts, pack, *refs):
    n = sum(counts)
    steps = len(counts)
    rows_in, cots_in = refs[:n], refs[n : 2 * n]
    outs, (w_in, w_down, row_buf, cot_buf, *scratch) = refs[2 * n : 2 * n + 4], refs[2 * n + 4 :]
    kept, (in_sem, out_sem) = scratch[:4], scratch[4:]
    grad_in, ffn_out, hidden_ref, both_ref = kept
    start_all(rows_in, counts, row_buf, in_sem.at[0])
    start_all(cots_in, counts, cot_buf, in_sem.at[1])
    size_z = pack.shape[0]
    model, ff = w_in.shape[0], w_down.shape[0]
    cell = 64
    seqs = model // (size_z * cell)
    fine = ff // size_z
    for z in range(size_z):
        for s in range(seqs):
            at = (s * size_z + z) * cell
            w_in[at : at + cell, :] = pack[z, s * cell : (s + 1) * cell, :]
        w_down[z * fine : (z + 1) * fine, :] = pack[z, seqs * cell :, :]

    @pl.loop(0, steps)
    def _(k):
        wait_for(row_buf.at[k], in_sem.at[0, k])
        wait_for(cot_buf.at[k], in_sem.at[1, k])
        both = dot(row_buf[k], w_in[...])
        gate, up = both[:, :ff], both[:, ff:]
        grad_hidden = dot_nt(cot_buf[k], w_down[...])
        sigma = 1.0 / (1.0 + jnp.exp(-gate))
        act = gate * sigma
        hidden = (act * up).astype(BF16)
        hidden_ref[k] = hidden
        both_ref[k, :, :ff] = (grad_hidden * up * (sigma + act * (1.0 - sigma))).astype(BF16)
        both_ref[k, :, ff:] = (grad_hidden * act).astype(BF16)
        grad_in[k] = dot_nt(both_ref[k], w_in[...]).astype(BF16)
        ffn_out[k] = dot(hidden, w_down[...]).astype(BF16)
        for index, (source, out) in enumerate(zip(kept, outs)):
            pltpu.make_async_copy(source.at[k], out.at[k], out_sem.at[index, k]).start()

    @pl.loop(0, steps)
    def _(k):
        for index, source in enumerate(kept):
            wait_for(source.at[k], out_sem.at[index, k])


def ffn(rows_parts, cot_parts, pack, order):
    counts = layout(rows_parts, order)
    pieces = flat(rows_parts, order) + flat(cot_parts, order)
    steps = len(order)
    row_count, width = rows_parts[0, 0, 0][0].shape
    _, _, both = pack.shape
    ff = both // 2
    wides = (width, width, ff, both)
    return pl.pallas_call(
        lambda *refs: ffn_kernel(counts, *refs),
        out_shape=tuple(shape_of((steps, row_count, wide)) for wide in wides),
        in_specs=[pl.BlockSpec(memory_space=pltpu.VMEM)] + [ANY] * len(pieces),
        out_specs=(ANY,) * 4,
        scratch_shapes=[pltpu.VMEM((width, both), BF16), pltpu.VMEM((ff, width), BF16)]
        + [pltpu.VMEM((steps, row_count, wide), BF16) for wide in (width, width, *wides)]
        + [pltpu.SemaphoreType.DMA((2, steps)), pltpu.SemaphoreType.DMA((4, steps))],
        cost_estimate=pl.CostEstimate(
            flops=2 * steps * row_count * width * ff * 6, bytes_accessed=12 * steps * row_count * width, transcendentals=steps * row_count * ff
        ),
        name="ffn",
    )(pack, *pieces)


def ffn_grads_kernel(n, *refs):
    rows_in, cots_in = refs[:n], refs[n : 2 * n]
    hids_in, boths_in = refs[2 * n : 2 * n + 2], refs[2 * n + 2 : 2 * n + 4]
    out, row_all, cot_all, hid_all, both_all, store, sem, out_sem = refs[2 * n + 4 :]
    size_z, ff, width = out.shape[0], hid_all.shape[2], row_all.shape[2]
    half = row_all.shape[1]
    cell = 64
    span = size_z * cell
    fine = ff // size_z

    def fetch(pieces, target, which):
        row = 0
        for ref in pieces:
            side, at = row // half, row % half
            pltpu.make_async_copy(ref, target.at[side, at : at + ref.shape[0]], sem.at[which, side]).start()
            row += ref.shape[0]

    middle = n // 2
    for side in range(2):
        sides = slice(side * middle, (side + 1) * middle)
        for which, pieces, target in ((0, rows_in[sides], row_all), (1, boths_in[side : side + 1], both_all)):
            row = 0
            for ref in pieces:
                pltpu.make_async_copy(ref, target.at[side, row : row + ref.shape[0]], sem.at[which, side]).start()
                row += ref.shape[0]
    for which, pieces, target in ((2, cots_in, cot_all), (3, hids_in, hid_all)):
        fetch(pieces, target, which)

    def left_part(left, right, side, cols):
        return dot_tn(left[side, :, cols], right[side])

    per = 2
    for group in range(width // (per * span)):
        cols = slice(group * per * span, (group + 1) * per * span)
        total = None
        for side in range(2):
            if group == 0:
                wait_for(row_all.at[side], sem.at[0, side])
                wait_for(both_all.at[side], sem.at[1, side])
            part = left_part(row_all, both_all, side, cols)
            total = part if total is None else total + part
        total = total.astype(BF16)
        for s in range(per):
            for z in range(size_z):
                at = s * span + z * cell
                store[z, (group * per + s) * cell : (group * per + s + 1) * cell, :] = total[at : at + cell]
        rows = slice(group * per * cell, (group + 1) * per * cell)
        pltpu.make_async_copy(store.at[:, rows], out.at[:, rows], out_sem.at[group]).start()
    groups = width // (per * span)
    total = None
    for side in range(2):
        wait_for(cot_all.at[side], sem.at[2, side])
        wait_for(hid_all.at[side], sem.at[3, side])
        part = left_part(hid_all, cot_all, side, slice(None))
        total = part if total is None else total + part
    total = total.astype(BF16)
    top = width // size_z
    for z in range(size_z):
        store[z, top:, :] = total[z * fine : (z + 1) * fine]
    pltpu.make_async_copy(store.at[:, top:], out.at[:, top:], out_sem.at[groups]).start()
    for group in range(groups):
        rows = slice(group * per * cell, (group + 1) * per * cell)
        pltpu.make_async_copy(store.at[:, rows], out.at[:, rows], out_sem.at[group]).wait()
    pltpu.make_async_copy(store.at[:, top:], out.at[:, top:], out_sem.at[groups]).wait()


def ffn_grads(rows_parts, cot_parts, hid_a, hid_b, both_a, both_b, size_z):
    order = SENT + KEPT
    rows_in, cots_in = flat(rows_parts, order), flat(cot_parts, order)
    width = rows_in[0].shape[1]
    half = sum(piece.shape[0] for piece in rows_in) // 2
    ff = hid_a.shape[-1]
    fine = ff // size_z
    flat2 = [a.reshape(half, a.shape[-1]) for a in (hid_a, hid_b, both_a, both_b)]
    shape = (size_z, width // size_z + fine, width)
    return pl.pallas_call(
        lambda *refs: ffn_grads_kernel(len(rows_in), *refs),
        out_shape=shape_of(shape),
        in_specs=[ANY] * (2 * len(rows_in) + 4),
        out_specs=ANY,
        scratch_shapes=[
            pltpu.VMEM((2, half, width), BF16),
            pltpu.VMEM((2, half, width), BF16),
            pltpu.VMEM((2, half, ff), BF16),
            pltpu.VMEM((2, half, 2 * ff), BF16),
            pltpu.VMEM(shape, BF16),
            pltpu.SemaphoreType.DMA((4, 2)),
            pltpu.SemaphoreType.DMA((4,)),
        ],
        cost_estimate=pl.CostEstimate(
            flops=12 * half * width * ff, bytes_accessed=20 * half * width, transcendentals=0
        ),
        name="ffn_grads",
    )(*rows_in, *cots_in, *flat2)


def scatter_plane(sent, kept):
    half = kept.shape[1] // 2
    came = swap(sent, "c")
    upper, lower = slice(0, half), slice(half, 2 * half)

    def total(blocks, rows):
        return kept[blocks, rows].astype(F32) + came[blocks, rows].astype(F32)

    to_x = total(slice(2, 4), upper).astype(BF16)
    to_y = total(slice(1, 4, 2), lower).astype(BF16)
    from_x, from_y = shift_x(to_x, 1), swap(to_y, "y")
    to_y = (total(1, upper) + from_x[1].astype(F32)).astype(BF16)
    to_x = (total(2, lower) + from_y[1].astype(F32)).astype(BF16)
    return [kept, came, from_x, from_y, swap(to_y, "y"), shift_x(to_x, 1)]


def scatter_direct(sent, kept):
    came = swap(sent, "c")
    to_y, to_x, to_d = [(kept[n].astype(F32) + came[n].astype(F32)).astype(BF16) for n in (1, 2, 3)]
    across = [(i, 3 - i) for i in range(4)]
    from_d = lax.ppermute(to_d, ("x", "y"), across)
    return [kept, came, swap(to_y, "y"), shift_x(to_x, 1), from_d]


def own_block(kept, came, from_x, from_y, last_y, last_x):
    half = last_y.shape[0]
    own = kept[...].astype(F32) + came[...].astype(F32)
    upper = own[:half] + from_x[...].astype(F32) + last_y[...].astype(F32)
    lower = own[half:] + from_y[...].astype(F32) + last_x[...].astype(F32)
    return jnp.concatenate([upper, lower], axis=0)


def with_own(kernel, outs, parts, others, flops=0):
    size = sum(math.prod(a.shape) * a.dtype.itemsize for a in (*outs, *others))

    def full(array):
        return pl.BlockSpec(array.shape, lambda i: (0,) * array.ndim)

    first = [
        pl.BlockSpec((None, *a.shape[1:]), lambda i: (0, 0, 0)) if a.ndim == 3 else full(a) for a in parts
    ]
    return pl.pallas_call(
        kernel,
        out_shape=tuple(outs),
        grid=(1,),
        in_specs=first + [full(a) for a in others],
        out_specs=tuple(full(a) for a in outs),
        cost_estimate=pl.CostEstimate(flops=flops, bytes_accessed=size, transcendentals=0),
    )(*parts, *others)


def block_out_kernel(*refs):
    parts, resid, out = refs[:6], refs[6], refs[7]
    out[...] = (resid[...] + own_block(*parts)).astype(BF16)


def ffn_back_kernel(*refs):
    parts, (resid, cot, gains, w_out, grad_resid, low, heads, gain_sum) = refs[:6], refs[6:]
    incoming = own_block(*parts)
    source = resid[...]
    grad_source, grad_gain = norm_back(incoming, source, gains[1:2, :])
    total = cot[...].astype(F32) + grad_source
    grad_resid[...] = total
    small = total.astype(BF16)
    low[...] = small
    gain_sum[...] = jnp.broadcast_to(grad_gain[None, :], gain_sum.shape)
    grads = dot_nt(small, w_out[...]).astype(BF16)
    width = heads.shape[2]
    for r in range(heads.shape[0]):
        heads[r] = grads[:, r * width : (r + 1) * width]


def input_back_kernel(*refs):
    parts, (tokens, gains, grad_resid, out) = refs[:6], refs[6:]
    grad_source, _ = norm_back(own_block(*parts), tokens[...].astype(F32), gains[0:1, :])
    out[...] = grad_resid[...] + grad_source


def out_grad_kernel(size_z, seq_ref, y_ref, attended, low, sent, kept, total):
    rows = sent.shape[1] // size_z
    total[...] = dot_tn(attended[...], low[...])
    for index in range(2 * sent.shape[0]):
        out = (sent, kept)[index // sent.shape[0]]
        for z in range(size_z):
            at = (seq_ref[index] * size_z + z) * 2 * rows + y_ref[index] * rows
            part = total[pl.ds(pl.multiple_of(at, rows), rows), :]
            out[index % sent.shape[0], z * rows : (z + 1) * rows, :] = part.astype(BF16)


def out_grad(seqs, ys, attended, low, size_z):
    width = attended.shape[1]
    full = pl.BlockSpec(memory_space=pltpu.VMEM)
    smem = pl.BlockSpec(memory_space=pltpu.SMEM)
    blocks = len(SENT)
    each = shape_of((blocks, width // (2 * blocks), width))
    return pl.pallas_call(
        lambda *refs: out_grad_kernel(size_z, *refs),
        out_shape=(each, each),
        in_specs=[smem, smem, full, full],
        out_specs=(full, full),
        scratch_shapes=[pltpu.VMEM((width, width), F32)],
        cost_estimate=pl.CostEstimate(
            flops=2 * attended.shape[0] * width * width, bytes_accessed=2 * width * width, transcendentals=0
        ),
        name="out_grad",
    )(seqs, ys, attended, low)


def attn_tail_kernel(rows, places, gains, gain_ffn, wo_kept, wo_came, wo_y, wo_x, wo_d, weight, grad_in, normed_in, sent, kept, sums, grad, normed, store, line_ref, sem, out_sem):
    steps = grad.shape[0]
    half = steps // 2
    for k in range(steps):
        pltpu.make_async_copy(grad_in.at[places[k]], grad.at[k], sem.at[0, k]).start()
        pltpu.make_async_copy(normed_in.at[places[k]], normed.at[k], sem.at[1, k]).start()
    share = jnp.zeros((8, normed.shape[2]), F32)
    line_ref[...] = share
    for side, out in enumerate((sent, kept)):

        @pl.loop(0, half)
        def _(i, side=side, out=out):
            k = i + side * half
            wait_for(grad.at[k], sem.at[0, k])
            wait_for(normed.at[k], sem.at[1, k])
            total = dot_nt(grad[k], weight[...])
            store[k] = total.astype(BF16)
            pltpu.make_async_copy(store.at[k], out.at[i], out_sem.at[k]).start()
            line_ref[...] += jnp.sum(
                (total * normed[k].astype(F32)).reshape(total.shape[0] // 8, 8, total.shape[1]), axis=0
            )

    size_z = sums.shape[0]
    wide = grad.shape[2]
    width = sums.shape[2] - wide
    model = normed.shape[2]
    cell = 64
    span = size_z * cell
    seqs = model // span
    all_normed = normed[...].reshape(-1, model)
    all_grad = grad[...].reshape(-1, wide)
    for s in range(seqs):
        total = dot_tn(all_normed[:, s * span : (s + 1) * span], all_grad).astype(BF16)
        for z in range(size_z):
            sums[z, s * cell : (s + 1) * cell, :wide] = total[z * cell : (z + 1) * cell]
    grad_out = sum((ref[0] if ref.shape != wo_d.shape else ref[...]).astype(F32) for ref in (wo_kept, wo_came, wo_y, wo_x, wo_d))
    grad_out = grad_out.astype(BF16)
    blocks = model // width
    end = blocks * rows
    both = (jnp.sum(line_ref[...], axis=0, keepdims=True) / gains[0:1, :], gain_ffn[0:1, :])
    for z in range(size_z):
        for r in range(blocks):
            sums[z, r * rows : (r + 1) * rows, wide:] = grad_out[
                z * rows : (z + 1) * rows, r * width : (r + 1) * width
            ]
        line = jnp.concatenate(
            [row[:, (q * size_z + z) * cell : (q * size_z + z + 1) * cell] for row in both for q in range(seqs)],
            axis=1,
        )
        sums[z, end:, :] = jnp.broadcast_to(line, (sums.shape[1] - end, line.shape[1])).astype(BF16)
    for k in range(steps):
        wait_for(store.at[k], out_sem.at[k])


def attn_tail(rows, places, gains, gain_ffn, grad_out, weight, grad, normed, size_z):
    steps, row_count, width = normed.shape
    wide = grad.shape[2]
    ranks = steps
    vmem = pl.BlockSpec(memory_space=pltpu.VMEM)
    half = shape_of((steps // 2, row_count, width))
    return pl.pallas_call(
        lambda *refs: attn_tail_kernel(rows, *refs),
        out_shape=(half, half, shape_of((size_z, ranks * rows + 16, wide + wide // 3))),
        in_specs=[pl.BlockSpec(memory_space=pltpu.SMEM)] + [vmem] * (3 + len(grad_out)) + [ANY, ANY],
        out_specs=(ANY, ANY, vmem),
        scratch_shapes=[
            pltpu.VMEM((steps, row_count, wide), BF16),
            pltpu.VMEM((steps, row_count, width), BF16),
            pltpu.VMEM((steps, row_count, width), BF16),
            pltpu.VMEM((8, width), F32),
            pltpu.SemaphoreType.DMA((2, steps)),
            pltpu.SemaphoreType.DMA((steps,)),
        ],
        cost_estimate=pl.CostEstimate(
            flops=4 * steps * row_count * width * wide, bytes_accessed=6 * steps * row_count * width, transcendentals=0
        ),
        name="attn_tail",
    )(places, gains, gain_ffn, *grad_out, weight, grad, normed)


def attn_unpack_kernel(rows, summed, payload, w_out):
    ranks, _, full = payload.shape
    width = full // 4
    wide = 3 * width
    for r in range(ranks):
        payload[r, :, :wide] = summed[r * rows : (r + 1) * rows, :wide]
        w_out[:, r * width : (r + 1) * width] = summed[r * rows : (r + 1) * rows, wide:].astype(F32)
        mine = [
            summed[ranks * rows : ranks * rows + 1, (n * ranks + r) * rows : (n * ranks + r + 1) * rows] for n in range(2)
        ]
        line = jnp.concatenate([*mine, jnp.zeros((1, width - 2 * rows), BF16)], axis=1)
        payload[r, :, wide:] = jnp.broadcast_to(line.astype(F32), (rows, width)).astype(BF16)


def attn_final_kernel(came, q, k, v, gains):
    ranks, _, full = came.shape
    width = full // 4
    total = jnp.zeros((8, width), F32)
    for r in range(ranks):
        for n, out in enumerate((q, k, v)):
            out[:, r * width : (r + 1) * width] = came[r, :, n * width : (n + 1) * width].astype(F32)
        total = total + came[r, 0:8, 3 * width :].astype(F32)
    gains[...] = total


def ffn_final_kernel(size_z, came, down, gate, up, down_out):
    ranks, _, both = came.shape
    ff = both // 2
    fine = ff // size_z
    for r in range(ranks):
        s, y = r // 2, r % 2
        for n, out in enumerate((gate, up)):
            for z in range(size_z):
                at = ((s * size_z + z) * 2 + y) * fine
                out[:, at : at + fine] = came[r, :, n * ff + z * fine : n * ff + (z + 1) * fine].astype(F32)
    down_out[...] = down[...].astype(F32)


def local_fast(
    tokens,
    w_query,
    w_key,
    w_value,
    w_out,
    gain_attn,
    w_gate,
    w_up,
    w_down,
    gain_ffn,
    counts,
    cotangent,
):
    size_x, size_z = lax.axis_size("x"), lax.axis_size("z")
    seq_ranks = 2 * size_x
    ranks = 2 * seq_ranks
    at_x, at_c, at_y = lax.axis_index("x"), lax.axis_index("c"), lax.axis_index("y")
    mine, cot_mine = tokens[0], cotangent[0]
    row_count, width = mine.shape
    rows = w_query.shape[0]
    head_width = width // ranks
    wide = 3 * head_width
    heads = HEADS // ranks
    ff = size_z * w_down.shape[0]
    seqs = jnp.stack([(at_x ^ dx) * 2 + (at_c ^ dc) for dc, dx, dy in SENT + KEPT]).astype(jnp.int32)
    ys = jnp.stack([at_y ^ dy for dc, dx, dy in SENT + KEPT]).astype(jnp.int32)
    places = ys * seq_ranks + seqs

    gains = jnp.pad(jnp.stack([gain_attn, gain_ffn], axis=1), ((0, 0), (0, head_width - 2)))
    first, second, out_pack = whole(
        lambda *refs: pack_kernel(size_z, *refs),
        [
            shape_of((ranks, rows, 4 * head_width)),
            shape_of((ranks, rows, 2 * ff)),
            shape_of((width // (4 * head_width) * rows, 4 * head_width)),
        ],
        [w_query, w_key, w_value, w_out, w_gate, w_up, gains],
    )
    first = all_to_all(first).reshape(ranks * rows, 4 * head_width)
    attn_pack = lax.all_gather(jnp.concatenate([first, out_pack], axis=0), "z", axis=0, tiled=False)
    early, _ = lax.optimization_barrier((mine, first))
    token_parts = gather_parts(early)
    my_length = jnp.sum(counts, axis=1)
    other_length = swap(my_length, "y")
    lens = jnp.where(at_y == 0, jnp.concatenate([my_length, other_length]), jnp.concatenate([other_length, my_length]))
    second, seqs, ys, places = lax.optimization_barrier((second, seqs, ys, places))
    second = all_to_all(second).reshape(ranks * rows, 2 * ff)
    second, lens = lax.optimization_barrier((second, lens))
    ffn_pack = lax.all_gather(jnp.concatenate([second, w_down], axis=0), "z", axis=0, tiled=False)
    later, _, _ = lax.optimization_barrier((cot_mine, token_parts[0, 1, 0][0], token_parts[0, 0, 1][0]))
    cot_parts = gather_parts(later)

    normed_attn, qkv, w_qkv, gains = norm_qkv(places, token_parts, attn_pack, wide)
    qkv = qkv.reshape(2, seq_ranks * row_count, wide)
    out_parts = gather_parts(out_block(attn_pack, ranks * rows, rows))
    w_out_full = out_weight(seqs, ys, out_parts, size_z)
    attended = attn_fwd(lens, qkv, heads, row_count)
    attended = all_to_all(attended.reshape(ranks, row_count, head_width))
    resid, normed_ffn, attended = whole(
        out_kernel,
        [shape_of((row_count, width), F32), shape_of((row_count, width)), shape_of((row_count, width))],
        [attended, mine, w_out_full, gains],
        flops=2 * row_count * width * width,
    )

    row_parts = gather_parts(normed_ffn)
    grad_sent, out_sent, hid_sent, both_sent = ffn(row_parts, cot_parts, ffn_pack, SENT)
    grad_kept, out_kept, hid_kept, both_kept = ffn(row_parts, cot_parts, ffn_pack, KEPT)
    grad_parts = scatter_plane(grad_sent, grad_kept)
    ffn_sums = ffn_grads(row_parts, cot_parts, hid_sent, hid_kept, both_sent, both_kept, size_z)
    ffn_sums = scatter_z(ffn_sums)

    token_f32 = shape_of((row_count, width), F32)
    grad_resid, resid_low, grad_heads, share_ffn = with_own(
        ffn_back_kernel,
        [token_f32, shape_of((row_count, width)), shape_of((ranks, row_count, head_width)), shape_of((8, width), F32)],
        grad_parts,
        [resid, cot_mine, gains, w_out_full],
        flops=2 * row_count * width * width,
    )
    grad_heads = all_to_all(grad_heads)
    grad_heads = grad_heads.reshape(seq_ranks, 2, row_count, head_width)
    wo_sent, wo_kept = out_grad(seqs, ys, attended, resid_low, size_z)
    wo_parts = scatter_direct(wo_sent, wo_kept)
    out_parts = scatter_plane(out_sent, out_kept)
    (block_output,) = with_own(block_out_kernel, [shape_of((row_count, width))], out_parts, [resid])

    grad_qkv = attn_bwd(lens, qkv, grad_heads, heads, row_count)
    by_block = grad_qkv.reshape(ranks, row_count, wide)
    back_sent, back_kept, attn_sums = attn_tail(
        rows, places, gains, share_ffn, wo_parts, w_qkv, by_block, normed_attn, size_z
    )
    back_parts = scatter_plane(back_sent, back_kept)
    attn_sums = scatter_z(attn_sums)
    (input_grad,) = with_own(input_back_kernel, [token_f32], back_parts, [mine, gains, grad_resid])

    ff_rows = w_down.shape[0]
    ffn_came = all_to_all(ffn_sums[: ranks * rows].reshape(ranks, rows, 2 * ff))
    big = shape_of((rows, ranks * ff), F32)
    grad_w_gate, grad_w_up, grad_w_down = whole(
        lambda *refs: ffn_final_kernel(size_z, *refs),
        [big, big, shape_of((ff_rows, width), F32)],
        [ffn_came, ffn_sums[ranks * rows :]],
    )
    each = shape_of((rows, width), F32)
    payload, grad_w_out = whole(
        lambda *refs: attn_unpack_kernel(rows, *refs), [shape_of((ranks, rows, 4 * head_width)), each], [attn_sums]
    )
    grad_w_query, grad_w_key, grad_w_value, gain_sums = whole(
        lambda *refs: attn_final_kernel(*refs),
        [each, each, each, shape_of((8, head_width), F32)],
        [all_to_all(payload)],
    )
    return (
        block_output[None],
        input_grad[None],
        grad_w_query,
        grad_w_key,
        grad_w_value,
        grad_w_out,
        gain_sums[0, :rows],
        grad_w_gate,
        grad_w_up,
        grad_w_down,
        gain_sums[0, rows : 2 * rows],
    )


def layer(*arrays):
    return local_fast(*arrays)


def solution(mesh):
    seq, batch = mesh.shape["seq"], mesh.shape["batch"]
    fine = Mesh(mesh.devices.reshape(seq // 2, 2, batch // 2, 2), ("x", "c", "z", "y"))
    token_spec = P(("z", "y"), ("x", "c"), None)
    row_spec = P(("x", "c", "z", "y"), None)
    gain_spec = P(("x", "c", "z", "y"))
    in_specs = (
        (token_spec,)
        + (row_spec,) * 4
        + (gain_spec,)
        + (row_spec,) * 3
        + (gain_spec, P(("z", "y"), None), token_spec)
    )
    out_specs = (
        (token_spec,) * 2
        + (row_spec,) * 4
        + (gain_spec,)
        + (row_spec,) * 3
        + (gain_spec,)
    )
    quick = fits(fine)
    return jax.shard_map(layer if quick else local_any, mesh=fine, in_specs=in_specs, out_specs=out_specs, check_vma=False)
```
